32 devices in a mesh: space: 16 (over z, x, core), tm: 2 (over y).
Axes of the slice: x: 2, y: 2, z: 4, core: 2. Of those that a mesh axis runs over, the one named last changes fastest.
Arguments:
- thermal_anomaly: bfloat16 [128, 140288], P('tm', 'space'), may hold values from -6 to 6
- smoothing_coefs: float32 [128], replicated, may hold values from -0.0075 to 0.0075
Outputs:
- orthonormal_basis: float32 [128, 140288], P(None, ('space', 'tm'))
- triangular_factor: float32 [128, 128], replicated
The draws below stay inside these ranges and needn't reach their ends.
All inputs are finite; a program needn't handle non-finite values.
Results may differ from the reference program's by a relative error of at most 0.0003.
The reference program's roundings to bfloat16 on the way count: a program that leaves them out, or rounds other values in their place, can miss the bound.
Values may be sent and summed in bfloat16 or wider, within the bound.
A program may use at most 64 MiB of HBM per device.

```python
import math
import jax
import jax.numpy as jnp
from jax import lax

TAPS = 129
SPAN_TIMESTEPS = 128
SPATIAL_SITES = 140288


def draw_thermal_anomaly(key, part):
    keys = jax.random.split(jax.random.fold_in(key, 17), 5)
    count = 6
    hours = jnp.arange(SPAN_TIMESTEPS, dtype=jnp.float32)[:, None]
    cycles = jax.random.uniform(keys[0], (count,), jnp.float32, 0.5, 8.0)
    phases = jax.random.uniform(keys[1], (count,), jnp.float32, -math.pi, math.pi)
    root_three = math.sqrt(3.0)
    patterns = jax.random.uniform(keys[3], (count, SPATIAL_SITES), jnp.float32, -root_three, root_three)
    strengths = jnp.exp(jax.random.uniform(keys[2], (count,), jnp.float32, math.log(0.12), math.log(0.35)))
    noise = jax.random.truncated_normal(keys[4], -3.0, 3.0, (SPAN_TIMESTEPS, SPATIAL_SITES), jnp.float32)
    total = noise
    for index in range(count):
        temporal = math.sqrt(2.0) * jnp.cos(2.0 * math.pi * cycles[index] * hours / SPAN_TIMESTEPS + phases[index])
        total = total + strengths[index] * temporal * patterns[index][None, :]
    return jnp.clip(total, -6.0, 6.0).astype(jnp.bfloat16)


def setup_inputs(seed: int = 0) -> dict:
    key_list = jax.random.split(jax.random.key(seed), 3)
    thermal_anomaly = draw_thermal_anomaly(jax.random.fold_in(key_list[2], 71), 0)
    smoothing_coefs = jnp.clip(jax.random.uniform(key_list[1], (TAPS - 1,), jnp.float32, -0.0075, 0.0075), -0.0075, 0.0075)
    return dict(thermal_anomaly=thermal_anomaly, smoothing_coefs=smoothing_coefs)


def banded_matrix(coefficients, count_rows, count_cols, delay_shift_amount):
    row_index = lax.broadcasted_iota(jnp.int32, (count_rows, count_cols), 0)
    col_index = lax.broadcasted_iota(jnp.int32, (count_rows, count_cols), 1)
    lag_index = row_index + delay_shift_amount - col_index
    length = coefficients.shape[0]
    inside = (lag_index >= 0) & (lag_index < length)
    safe = jnp.clip(lag_index, 0, length - 1).astype(jnp.int32)
    return jnp.where(inside, coefficients[safe], jnp.zeros((), coefficients.dtype))

def reference(thermal_anomaly, smoothing_coefs):
    coefficients = jnp.concatenate([jnp.ones((1,), jnp.float32), smoothing_coefs.astype(jnp.float32)]).astype(jnp.bfloat16)
    snapshot_array = banded_matrix(coefficients, SPAN_TIMESTEPS, SPAN_TIMESTEPS, 0)
    averaged_record = jnp.dot(snapshot_array.astype(jnp.float32), thermal_anomaly.astype(jnp.float32), preferred_element_type=jnp.float32).astype(jnp.bfloat16)
    gram = jnp.dot(averaged_record.astype(jnp.float32), averaged_record.T.astype(jnp.float32), preferred_element_type=jnp.float32)
    lower_one = jnp.linalg.cholesky(gram)
    first_rows = jax.scipy.linalg.solve_triangular(lower_one, averaged_record.astype(jnp.float32), lower=True)
    scale = jnp.sqrt(jnp.float32(SPATIAL_SITES))
    return (first_rows * scale, lower_one / scale)
```

```python
import functools
import math

import jax
import jax.numpy as jnp
from jax import lax
from jax.experimental import pallas as pl
from jax.experimental.pallas import tpu as pltpu
from jax.sharding import PartitionSpec as P

LANES = 128
SUB = 8
PLANE = 4
CHUNKS = 5
SLABS = 4
GRANT = 16 * 2**20
MESH = pl.DeviceIdType.MESH


def banded(coefficients, rows, cols, delay):
    lag = (
        lax.broadcasted_iota(jnp.int32, (rows, cols), 0)
        + delay
        - lax.broadcasted_iota(jnp.int32, (rows, cols), 1)
    )
    one_hot = lag[:, :, None] == lax.broadcasted_iota(
        jnp.int32, (1, 1, coefficients.shape[0]), 2
    )
    return jnp.sum(jnp.where(one_hot, coefficients.astype(jnp.float32), 0.0), axis=2).astype(
        coefficients.dtype
    )


def general_body(thermal_anomaly, smoothing_coefs):
    steps = thermal_anomaly.shape[0]
    blocks = lax.axis_size("tm")
    coefficients = jnp.concatenate([jnp.ones((1,), jnp.float32), smoothing_coefs]).astype(
        jnp.bfloat16
    )
    reach = min(blocks - 1, -(-(coefficients.shape[0] - 1) // steps))
    record = [thermal_anomaly]
    for distance in range(1, reach + 1):
        route = [(i, i + distance) for i in range(blocks - distance)]
        record.insert(0, lax.ppermute(thermal_anomaly, "tm", route))
    matrix = banded(coefficients, steps, (reach + 1) * steps, reach * steps)
    outgoing = jnp.dot(
        matrix, jnp.concatenate(record, axis=0), preferred_element_type=jnp.float32
    ).astype(jnp.bfloat16)
    arrived = lax.all_to_all(outgoing, "tm", split_axis=1, concat_axis=0, tiled=True)
    gram = lax.psum(
        jnp.dot(arrived, arrived.T, preferred_element_type=jnp.float32), ("space", "tm")
    )
    lower = jnp.linalg.cholesky(gram)
    rows = jax.scipy.linalg.solve_triangular(lower, arrived.astype(jnp.float32), lower=True)
    scale = jnp.sqrt(jnp.float32(thermal_anomaly.shape[1] * lax.axis_size("space")))
    return rows * scale, lower / scale


def place(dst, rows, x_ref, base, start, width, half):
    valid = min(width, half - start)
    low = base + start
    aligned = low // LANES * LANES
    shift = low - aligned
    end = min(aligned + pl.cdiv(shift + valid, LANES) * LANES, x_ref.shape[1])
    value = x_ref[:, aligned:end][:, shift : shift + valid]
    if valid < width:
        edge = valid // LANES * LANES
        dst[rows, start + edge : start + width] = jnp.zeros(
            (value.shape[0], width - edge), dst.dtype
        )
    dst[rows, start : start + valid] = value


def gather_kernel(
    spans,
    x_hbm,
    coef_hbm,
    filtered_hbm,
    gram_ref,
    x_ref,
    coef_ref,
    filtered_ref,
    load_sem,
    store_sem,
    outgoing,
    panel,
    partial,
    pieces,
    reduced,
    planes,
    whole,
    swap_send,
    swap_recv,
    rs_send,
    rs_recv,
    line_send,
    line_recv,
    ag_send,
    ag_recv,
):
    space = lax.axis_index("space")
    tm = lax.axis_index("tm")
    inner = space % PLANE
    plane = space // PLANE
    lines = lax.axis_size("space") // PLANE
    group = PLANE * 2
    me = inner * 2 + tm
    hours = x_ref.shape[0]
    total = 2 * hours
    half = x_ref.shape[1] // 2
    share = total // group

    def in_group(offset):
        other = (me + offset) % group
        return other, (plane * PLANE + other // 2, other % 2)

    def in_line(offset):
        return ((plane + offset) % lines * PLANE + inner, tm)

    barrier = pltpu.get_barrier_semaphore()
    for offset in range(1, group):
        pl.semaphore_signal(barrier, inc=1, device_id=in_group(offset)[1], device_id_type=MESH)
    for offset in range(1, lines):
        pl.semaphore_signal(barrier, inc=1, device_id=in_line(offset), device_id_type=MESH)

    slab = hours // SLABS
    loads = [
        pltpu.make_async_copy(
            x_hbm.at[pl.ds(slab * index, slab)],
            x_ref.at[pl.ds(slab * index, slab)],
            load_sem.at[index],
        )
        for index in range(SLABS)
    ] + [pltpu.make_async_copy(coef_hbm, coef_ref, load_sem.at[SLABS])]
    for copy in loads:
        copy.start()
    for copy in loads:
        copy.wait()

    swaps = []
    for index, (start, width) in enumerate(spans):
        for side in range(2):

            @pl.when(tm == side)
            def _():
                place(outgoing, slice(None), x_ref, (1 - side) * half, start, width, half)

        if index == 0:
            pl.semaphore_wait(barrier, group - 1 + lines - 1)
        copy = pltpu.make_async_remote_copy(
            src_ref=outgoing.at[:, pl.ds(start, width)],
            dst_ref=panel.at[pl.ds(pl.multiple_of(tm * hours, hours), hours), pl.ds(start, width)],
            send_sem=swap_send.at[index],
            recv_sem=swap_recv.at[index],
            device_id=(space, 1 - tm),
            device_id_type=MESH,
        )
        copy.start()
        swaps.append(copy)

    for side in range(2):

        @pl.when(tm == side)
        def _():
            rows = slice(side * hours, (side + 1) * hours)
            for start, width in spans:
                place(panel, rows, x_ref, side * half, start, width, half)

    row = lax.broadcasted_iota(jnp.int32, (total, total), 0)
    col = lax.broadcasted_iota(jnp.int32, (total, total), 1)
    lagged = jnp.broadcast_to(coef_ref[...], (total, total))
    lagged = pltpu.roll(lagged, 1, axis=1, stride=1, stride_axis=0)
    turned = jnp.where(col > row, lagged, jnp.where(col == row, 1.0, 0.0))
    matrix = turned.T.astype(jnp.bfloat16)

    stores = []
    partial[...] = jnp.zeros_like(partial)
    for index, (start, width) in enumerate(spans):
        swaps[index].wait_recv()
        values = jnp.dot(
            matrix, panel[:, start : start + width], preferred_element_type=jnp.float32
        ).astype(jnp.bfloat16)
        filtered_ref[start : start + width, :] = values.T
        store = pltpu.make_async_copy(
            filtered_ref.at[pl.ds(start, width)],
            filtered_hbm.at[pl.ds(start, width)],
            store_sem.at[index],
        )
        store.start()
        stores.append(store)
        partial[...] += lax.dot_general(
            values, values, (((1,), (1,)), ((), ())), preferred_element_type=jnp.float32
        )

    copies = []
    for offset in range(1, group):
        other, device = in_group(offset)
        copy = pltpu.make_async_remote_copy(
            src_ref=partial.at[pl.ds(pl.multiple_of(other * share, share), share)],
            dst_ref=pieces.at[offset - 1],
            send_sem=rs_send.at[offset - 1],
            recv_sem=rs_recv.at[offset - 1],
            device_id=device,
            device_id_type=MESH,
        )
        copy.start()
        copies.append(copy)
    mine = pl.ds(pl.multiple_of(me * share, share), share)
    running = partial[mine, :]
    for offset in range(1, group):
        copies[offset - 1].wait_recv()
        running = running + pieces[offset - 1]
    reduced[...] = running
    planes[plane] = running

    for offset in range(1, lines):
        copy = pltpu.make_async_remote_copy(
            src_ref=reduced,
            dst_ref=planes.at[plane],
            send_sem=line_send.at[offset - 1],
            recv_sem=line_recv.at[offset - 1],
            device_id=in_line(offset),
            device_id_type=MESH,
        )
        copy.start()
        copies.append(copy)
    for offset in range(1, lines):
        copies[group - 1 + offset - 1].wait_recv()
    running = planes[0]
    for index in range(1, lines):
        running = running + planes[index]
    whole[mine, :] = running

    for offset in range(1, group):
        copy = pltpu.make_async_remote_copy(
            src_ref=whole.at[mine],
            dst_ref=whole.at[mine],
            send_sem=ag_send.at[offset - 1],
            recv_sem=ag_recv.at[offset - 1],
            device_id=in_group(offset)[1],
            device_id_type=MESH,
        )
        copy.start()
        copies.append(copy)
    for copy in copies[-(group - 1) :]:
        copy.wait_recv()
    gram_ref[...] = whole[...]
    for copy in swaps + copies:
        copy.wait_send()
    for store in stores:
        store.wait()


def factor(gram_ref, store):
    size = gram_ref.shape[0]
    count = size // SUB
    full = (SUB, size)
    blocks = [gram_ref[SUB * b : SUB * (b + 1), :] for b in range(count)]
    lane = lax.broadcasted_iota(jnp.int32, full, 1)
    sub = lax.broadcasted_iota(jnp.int32, full, 0)
    for b in range(count):
        first = b * SUB
        inside = (lane >= first) & (lane < first + SUB)
        columns = [
            [jnp.broadcast_to(blocks[i][:, first + c : first + c + 1], full) for c in range(SUB)]
            for i in range(b, count)
        ]
        upper = [
            [
                jnp.broadcast_to(columns[0][c][r : r + 1, :], full) if c >= r else None
                for c in range(SUB)
            ]
            for r in range(SUB)
        ]
        rows = [
            jnp.where(
                inside,
                jnp.where(lane == first + r, 1.0, 0.0),
                jnp.broadcast_to(blocks[b][r : r + 1, :], full),
            )
            for r in range(SUB)
        ]
        unit = [[None] * SUB for _ in range(SUB)]
        inverse = [None] * SUB
        for c in range(SUB):
            inverse[c] = 1.0 / upper[c][c]
            for r in range(c + 1, SUB):
                unit[c][r] = upper[c][r] * inverse[c]
                for j in range(r, SUB):
                    upper[r][j] = upper[r][j] - unit[c][r] * upper[c][j]
                rows[r] = rows[r] - unit[c][r] * rows[c]
        store(b, rows, upper, lane, sub)
        solved = [rows[r] * inverse[r] for r in range(SUB)]
        for c in range(SUB - 1, 0, -1):
            for r in range(c):
                solved[r] = solved[r] - unit[r][c] * solved[c]
        for i in range(b + 1, count):
            terms = [columns[i - b][c] * solved[c] for c in range(SUB)]
            while len(terms) > 1:
                terms = [terms[t] + terms[t + 1] for t in range(0, len(terms), 2)]
            blocks[i] = jnp.where(inside, 0.0, blocks[i]) - terms[0]


def basis_kernel(
    points,
    spans,
    gram_ref,
    filtered_hbm,
    basis_hbm,
    factor_hbm,
    filtered_ref,
    basis_ref,
    factor_ref,
    split,
    turned,
    load_sem,
    store_sem,
):
    size = gram_ref.shape[0]
    load = pltpu.make_async_copy(filtered_hbm, filtered_ref, load_sem)
    load.start()
    root = math.sqrt(points)

    def store(b, rows, upper, lane, sub):
        first = b * SUB
        block = rows[0]
        pivot = upper[0][0]
        for r in range(1, SUB):
            block = jnp.where(sub == r, rows[r], block)
            pivot = jnp.where(sub == r, upper[r][r], pivot)
        corner = block
        for r in range(SUB):
            for c in range(r, SUB):
                corner = jnp.where((sub == r) & (lane == first + c), upper[r][c], corner)
        diagonal = jnp.sqrt(pivot)
        here = slice(first, first + SUB)
        inverse = jnp.where(lane <= sub + first, block, 0.0) * (root / diagonal)
        top = inverse.astype(jnp.bfloat16).astype(jnp.float32)
        split[here, :] = top
        split[size + first : size + first + SUB, :] = inverse - top
        turned[here, :] = jnp.where(lane >= sub + first, corner, 0.0) / (diagonal * root)

    factor(gram_ref, store)
    load.wait()
    both_parts = split[...].astype(jnp.bfloat16)
    stores = []
    for index, (start, width) in enumerate(spans):
        rows = pl.ds(start, min(width, basis_ref.shape[0] - start))
        both = lax.dot_general(
            filtered_ref[rows, :],
            both_parts,
            (((1,), (1,)), ((), ())),
            preferred_element_type=jnp.float32,
        )
        basis_ref[rows, :] = both[:, :size] + both[:, size:]
        copy = pltpu.make_async_copy(
            basis_ref.at[rows], basis_hbm.at[rows], store_sem.at[index]
        )
        copy.start()
        stores.append(copy)
        if index == 0:
            factor_ref[...] = turned[...].T
            copy = pltpu.make_async_copy(factor_ref, factor_hbm, store_sem.at[len(spans)])
            copy.start()
            stores.append(copy)
    for copy in stores:
        copy.wait()


def paired_body(thermal_anomaly, smoothing_coefs):
    hours, sites = thermal_anomaly.shape
    total = 2 * hours
    half = sites // 2
    tiles = pl.cdiv(half, LANES)
    edge = max(1, tiles // (2 * CHUNKS))
    step = max(1, pl.cdiv(tiles - 2 * edge, CHUNKS - 2))
    cuts = [0, *range(edge, max(edge, tiles - edge), step), max(edge, tiles - edge), tiles]
    spans = [(a * LANES, (b - a) * LANES) for a, b in zip(cuts, cuts[1:]) if b > a]
    padded = tiles * LANES
    group = PLANE * 2
    lines = lax.axis_size("space") // PLANE
    share = total // group
    dma = pltpu.SemaphoreType.DMA
    vmem = pl.BlockSpec(memory_space=pltpu.VMEM)
    anywhere = pl.BlockSpec(memory_space=pl.ANY)
    filtered, gram = pl.pallas_call(
        functools.partial(gather_kernel, spans),
        out_shape=(
            jax.ShapeDtypeStruct((padded, total), jnp.bfloat16),
            jax.ShapeDtypeStruct((total, total), jnp.float32),
        ),
        in_specs=[pl.BlockSpec(memory_space=pltpu.HBM)] * 2,
        out_specs=(anywhere, vmem),
        scratch_shapes=[
            pltpu.VMEM((hours, sites), jnp.bfloat16),
            pltpu.VMEM((1, total), jnp.float32),
            pltpu.VMEM((padded, total), jnp.bfloat16),
            dma((SLABS + 1,)),
            dma((len(spans),)),
            pltpu.VMEM((hours, padded), jnp.bfloat16),
            pltpu.VMEM((total, padded), jnp.bfloat16),
            pltpu.VMEM((total, total), jnp.float32),
            pltpu.VMEM((group - 1, share, total), jnp.float32),
            pltpu.VMEM((share, total), jnp.float32),
            pltpu.VMEM((lines, share, total), jnp.float32),
            pltpu.VMEM((total, total), jnp.float32),
            dma((len(spans),)),
            dma((len(spans),)),
            dma((group - 1,)),
            dma((group - 1,)),
            dma((lines - 1,)),
            dma((lines - 1,)),
            dma((group - 1,)),
            dma((group - 1,)),
        ],
        compiler_params=pltpu.CompilerParams(
            collective_id=0, has_side_effects=True, vmem_limit_bytes=GRANT
        ),
        name="gather_gram",
    )(
        pltpu.with_memory_space_constraint(thermal_anomaly, pltpu.HBM),
        pltpu.with_memory_space_constraint(smoothing_coefs[:total].reshape(1, total), pltpu.HBM),
    )

    points = sites * lax.axis_size("space")
    basis, lower = pl.pallas_call(
        functools.partial(basis_kernel, points, spans),
        out_shape=(
            jax.ShapeDtypeStruct((half, total), jnp.float32),
            jax.ShapeDtypeStruct((total, total), jnp.float32),
        ),
        in_specs=[vmem, anywhere],
        out_specs=(anywhere, anywhere),
        scratch_shapes=[
            pltpu.VMEM((padded, total), jnp.bfloat16),
            pltpu.VMEM((half, total), jnp.float32),
            pltpu.VMEM((total, total), jnp.float32),
            pltpu.VMEM((2 * total, total), jnp.float32),
            pltpu.VMEM((total, total), jnp.float32),
            dma,
            dma((len(spans) + 1,)),
        ],
        compiler_params=pltpu.CompilerParams(vmem_limit_bytes=GRANT),
        name="factor_basis",
    )(gram, filtered)
    return basis.T, lower


def body(thermal_anomaly, smoothing_coefs):
    hours, sites = thermal_anomaly.shape
    paired = (
        lax.axis_size("tm") == 2
        and 2 * hours == LANES
        and smoothing_coefs.shape[0] >= LANES
        and sites % 2 == 0
        and lax.axis_size("space") % PLANE == 0
        and lax.axis_size("space") > PLANE
    )
    return (paired_body if paired else general_body)(thermal_anomaly, smoothing_coefs)


def solution(mesh):
    placed = (P("tm", "space"), P())
    return jax.shard_map(
        body, mesh=mesh, in_specs=placed, out_specs=(P(None, ("space", "tm")), P()), check_vma=False
    )
```

```python
import functools
import math

import jax
import jax.numpy as jnp
from jax import lax
from jax.experimental import pallas as pl
from jax.experimental.pallas import tpu as pltpu
from jax.sharding import PartitionSpec as P

LANES = 128
SUB = 8
PLANE = 4
CHUNKS = 5
FIRST = 17 * LANES
FAR_FIRST = (7, 5, 3, 1, 6, 4, 2)
LINE_AFTER = 0
GATHER_AFTER = 1
SPLIT = 4
GRANT = 16 * 2**20
MESH = pl.DeviceIdType.MESH


def banded(coefficients, rows, cols, delay):
    lag = (
        lax.broadcasted_iota(jnp.int32, (rows, cols), 0)
        + delay
        - lax.broadcasted_iota(jnp.int32, (rows, cols), 1)
    )
    one_hot = lag[:, :, None] == lax.broadcasted_iota(
        jnp.int32, (1, 1, coefficients.shape[0]), 2
    )
    return jnp.sum(jnp.where(one_hot, coefficients.astype(jnp.float32), 0.0), axis=2).astype(
        coefficients.dtype
    )


def general_body(thermal_anomaly, smoothing_coefs):
    steps = thermal_anomaly.shape[0]
    blocks = lax.axis_size("tm")
    coefficients = jnp.concatenate([jnp.ones((1,), jnp.float32), smoothing_coefs]).astype(
        jnp.bfloat16
    )
    reach = min(blocks - 1, -(-(coefficients.shape[0] - 1) // steps))
    record = [thermal_anomaly]
    for distance in range(1, reach + 1):
        route = [(i, i + distance) for i in range(blocks - distance)]
        record.insert(0, lax.ppermute(thermal_anomaly, "tm", route))
    matrix = banded(coefficients, steps, (reach + 1) * steps, reach * steps)
    outgoing = jnp.dot(
        matrix, jnp.concatenate(record, axis=0), preferred_element_type=jnp.float32
    ).astype(jnp.bfloat16)
    arrived = lax.all_to_all(outgoing, "tm", split_axis=1, concat_axis=0, tiled=True)
    gram = lax.psum(
        jnp.dot(arrived, arrived.T, preferred_element_type=jnp.float32), ("space", "tm")
    )
    lower = jnp.linalg.cholesky(gram)
    rows = jax.scipy.linalg.solve_triangular(lower, arrived.astype(jnp.float32), lower=True)
    scale = jnp.sqrt(jnp.float32(thermal_anomaly.shape[1] * lax.axis_size("space")))
    return rows * scale, lower / scale


def gather_kernel(
    spans,
    x_hbm,
    coef_hbm,
    filtered_ref,
    late_ref,
    early_ref,
    x_ref,
    coef_ref,
    tail,
    panel,
    partial,
    pieces,
    reduced,
    planes,
    first_partial,
    first_pieces,
    first_reduced,
    first_planes,
    first_whole,
    whole,
    load_sem,
    swap_send,
    swap_recv,
    rs_send,
    rs_recv,
    line_send,
    line_recv,
    ag_send,
    ag_recv,
    first_rs_send,
    first_rs_recv,
    first_line_send,
    first_line_recv,
    first_ag_send,
    first_ag_recv,
):
    space = lax.axis_index("space")
    tm = lax.axis_index("tm")
    inner = space % PLANE
    plane = space // PLANE
    lines = lax.axis_size("space") // PLANE
    group = PLANE * 2
    me = inner * 2 + tm
    hours, sites = x_ref.shape
    total = 2 * hours
    half = sites // 2
    low = half // LANES * LANES
    shift = half - low
    full = panel.shape[1] - LANES
    share = hours // group
    quarter = first_partial.shape[0] // PLANE

    def in_group(k):
        x = inner // 2
        core = inner % 2
        x = 1 - x if k & 4 else x
        core = 1 - core if k & 2 else core
        side = 1 - tm if k & 1 else tm
        near = x * 2 + core
        return near * 2 + side, (plane * PLANE + near, side)

    def in_line(offset):
        return ((plane + offset) % lines * PLANE + inner, tm)

    barrier = pltpu.get_barrier_semaphore()
    for offset in range(1, lines):
        pl.semaphore_signal(barrier, inc=1, device_id=in_line(offset), device_id_type=MESH)
    for k in FAR_FIRST:
        pl.semaphore_signal(barrier, inc=1, device_id=in_group(k)[1], device_id_type=MESH)

    own = pl.ds(pl.multiple_of(tm * hours, hours), hours)
    load_x = pltpu.make_async_copy(x_hbm, x_ref, load_sem.at[0])
    load_coef = pltpu.make_async_copy(coef_hbm, coef_ref, load_sem.at[1])
    load_own = pltpu.make_async_copy(
        x_hbm.at[:, pl.ds(pl.multiple_of(tm * low, LANES), full)],
        panel.at[own, pl.ds(0, full)],
        load_sem.at[2],
    )
    for copy in (load_x, load_coef, load_own):
        copy.start()

    pl.semaphore_wait(barrier, group - 1 + lines - 1)
    swaps = []
    for index, (start, width) in enumerate(spans):
        copy = pltpu.make_async_remote_copy(
            src_ref=x_hbm.at[
                :, pl.ds(pl.multiple_of((1 - tm) * low + start, LANES), width)
            ],
            dst_ref=panel.at[own, pl.ds(start, width)],
            send_sem=swap_send.at[index],
            recv_sem=swap_recv.at[index],
            device_id=(space, 1 - tm),
            device_id_type=MESH,
        )
        swaps.append(copy)
    for copy in swaps[:-1]:
        copy.start()

    load_x.wait()
    for side in range(2):

        @pl.when(tm == side)
        def _():
            for target, to in ((tail, 1 - side), (None, side)):
                begin = to * low + full
                width = min(LANES, sites - begin)
                value = x_ref[:, begin : begin + width]
                if width < LANES:
                    pad = jnp.zeros((hours, LANES - width), value.dtype)
                    value = jnp.concatenate([value, pad], axis=1)
                if target is None:
                    panel[side * hours : (side + 1) * hours, full : full + LANES] = value
                else:
                    target[...] = value

    tail_copy = pltpu.make_async_remote_copy(
        src_ref=tail,
        dst_ref=panel.at[own, pl.ds(full, LANES)],
        send_sem=swap_send.at[len(spans)],
        recv_sem=swap_recv.at[len(spans)],
        device_id=(space, 1 - tm),
        device_id_type=MESH,
    )
    tail_copy.start()
    swaps[-1].start()

    load_coef.wait()
    row = lax.broadcasted_iota(jnp.int32, (total, total), 0)
    col = lax.broadcasted_iota(jnp.int32, (total, total), 1)
    lagged = jnp.broadcast_to(coef_ref[...], (total, total))
    lagged = pltpu.roll(lagged, 1, axis=1, stride=1, stride_axis=0)
    turned = jnp.where(col > row, lagged, jnp.where(col == row, 1.0, 0.0))
    matrix = turned.T.astype(jnp.bfloat16)
    corner = matrix[:hours, :hours]

    def first_near(offset):
        near = (inner + offset) % PLANE
        return near, plane * PLANE + near

    def first_scatter(offset):
        near, other = first_near(offset)
        return pltpu.make_async_remote_copy(
            src_ref=first_partial.at[pl.ds(pl.multiple_of(near * quarter, quarter), quarter)],
            dst_ref=first_pieces.at[offset - 1],
            send_sem=first_rs_send.at[offset - 1],
            recv_sem=first_rs_recv.at[offset - 1],
            device_id=(other, tm),
            device_id_type=MESH,
        )

    def first_line(offset):
        return pltpu.make_async_remote_copy(
            src_ref=first_reduced,
            dst_ref=first_planes.at[plane],
            send_sem=first_line_send.at[offset - 1],
            recv_sem=first_line_recv.at[offset - 1],
            device_id=in_line(offset),
            device_id_type=MESH,
        )

    first_mine = pl.ds(pl.multiple_of(inner * quarter, quarter), quarter)

    def first_gather(offset, side):
        return pltpu.make_async_remote_copy(
            src_ref=first_whole.at[first_mine],
            dst_ref=first_whole.at[first_mine],
            send_sem=first_ag_send.at[side * PLANE + offset],
            recv_sem=first_ag_recv.at[offset],
            device_id=(first_near(offset)[1], side),
            device_id_type=MESH,
        )

    @pl.when(tm == 0)
    def _():
        gram = jnp.zeros((hours, hours), jnp.float32)
        cuts = [*range(0, low + full, FIRST), low + full]
        parts = [x_ref[:, a:b] for a, b in zip(cuts, cuts[1:])] + [tail[...]]
        for part in parts:
            values = jnp.dot(corner, part, preferred_element_type=jnp.float32).astype(jnp.bfloat16)
            gram = gram + lax.dot_general(
                values, values, (((1,), (1,)), ((), ())), preferred_element_type=jnp.float32
            )
        first_partial[...] = jnp.concatenate([gram[: hours // 2], gram[hours // 2 :]], axis=1)
        for offset in range(1, PLANE):
            first_scatter(offset).start()

    def first_stage_line():
        @pl.when(tm == 0)
        def _():
            running = first_partial[first_mine, :]
            for offset in range(1, PLANE):
                first_scatter(offset).wait_recv()
                running = running + first_pieces[offset - 1]
            first_reduced[...] = running
            first_planes[plane] = running
            for offset in range(1, lines):
                first_line(offset).start()

    def first_stage_gather():
        @pl.when(tm == 0)
        def _():
            for offset in range(1, lines):
                first_line(offset).wait_recv()
            running = first_planes[0]
            for index in range(1, lines):
                running = running + first_planes[index]
            first_whole[first_mine, :] = running
            for side in (1, 0):
                for offset in range(PLANE):
                    if side or offset:
                        first_gather(offset, side).start()

    load_own.wait()
    partial[...] = jnp.zeros_like(partial)
    for index, (start, width) in enumerate(spans):
        swaps[index].wait_recv()
        if index == len(spans) - 1:
            tail_copy.wait_recv()
            width += LANES
        values = jnp.dot(
            matrix, panel[:, start : start + width], preferred_element_type=jnp.float32
        )
        if start < shift or start + width > half:
            point = lax.broadcasted_iota(jnp.int32, (total, width), 1) + (start - tm * shift)
            values = jnp.where((point >= 0) & (point < half), values, 0.0)
        values = values.astype(jnp.bfloat16)
        filtered_ref[start : start + width, :] = values.T
        partial[...] += lax.dot_general(
            values[hours:], values, (((1,), (1,)), ((), ())), preferred_element_type=jnp.float32
        )
        if index == min(LINE_AFTER, len(spans) - 2):
            first_stage_line()
        if index == min(GATHER_AFTER, len(spans) - 2):
            first_stage_gather()

    copies = []
    for k in FAR_FIRST:
        other, device = in_group(k)
        copy = pltpu.make_async_remote_copy(
            src_ref=partial.at[pl.ds(pl.multiple_of(other * share, share), share)],
            dst_ref=pieces.at[k - 1],
            send_sem=rs_send.at[k - 1],
            recv_sem=rs_recv.at[k - 1],
            device_id=device,
            device_id_type=MESH,
        )
        copy.start()
        copies.append(copy)

    @pl.when(tm == 0)
    def _():
        for offset in range(1, PLANE):
            first_gather(offset, 0).wait_recv()

    @pl.when(tm == 1)
    def _():
        for offset in range(PLANE):
            first_gather(offset, 1).wait_recv()

    blank = jnp.zeros((SUB, hours), jnp.float32)
    blocks = []
    for b in range(hours // SUB):
        begin = b * SUB
        packed = first_whole[begin % (hours // 2) : begin % (hours // 2) + SUB, :]
        side = begin // (hours // 2)
        blocks.append(
            jnp.concatenate([packed[:, side * hours : (side + 1) * hours], blank], axis=1)
        )

    def store(first, rows, upper, lane, sub):
        block, pivot, corner = assemble(first, rows, upper, lane, sub)
        diagonal = jnp.sqrt(pivot)
        early_ref[first : first + SUB, :] = (
            jnp.where(lane <= sub + first, block, 0.0) / diagonal
        )
        early_ref[hours + first : hours + first + SUB, :] = (
            jnp.where(lane >= sub + first, corner, 0.0) / diagonal
        )

    for b in range(SPLIT):
        eliminate(blocks, b, 0, store)

    mine = pl.ds(pl.multiple_of(me * share, share), share)
    running = partial[mine, :]
    for k, copy in zip(FAR_FIRST, copies):
        copy.wait_recv()
        running = running + pieces[k - 1]
    reduced[...] = running
    planes[plane] = running

    for offset in range(1, lines):
        copy = pltpu.make_async_remote_copy(
            src_ref=reduced,
            dst_ref=planes.at[plane],
            send_sem=line_send.at[offset - 1],
            recv_sem=line_recv.at[offset - 1],
            device_id=in_line(offset),
            device_id_type=MESH,
        )
        copy.start()
        copies.append(copy)
    for b in range(SPLIT, len(blocks)):
        eliminate(blocks, b, 0, store)
    for copy in copies[group - 1 :]:
        copy.wait_recv()
    running = planes[0]
    for index in range(1, lines):
        running = running + planes[index]
    whole[mine, :] = running

    for k in FAR_FIRST:
        copy = pltpu.make_async_remote_copy(
            src_ref=whole.at[mine],
            dst_ref=whole.at[mine],
            send_sem=ag_send.at[k - 1],
            recv_sem=ag_recv.at[k - 1],
            device_id=in_group(k)[1],
            device_id_type=MESH,
        )
        copy.start()
        copies.append(copy)
    for copy in swaps + [tail_copy] + copies[: -(group - 1)]:
        copy.wait_send()

    @pl.when(tm == 0)
    def _():
        for offset in range(1, PLANE):
            first_scatter(offset).wait_send()
        for offset in range(1, lines):
            first_line(offset).wait_send()
        for side in (1, 0):
            for offset in range(PLANE):
                if side or offset:
                    first_gather(offset, side).wait_send()

    for copy in copies[-(group - 1) :]:
        copy.wait_recv()
    late_ref[...] = whole[...]
    for copy in copies[-(group - 1) :]:
        copy.wait_send()


def assemble(first, rows, upper, lane, sub):
    block = rows[0]
    pivot = upper[0][0]
    for r in range(1, SUB):
        block = jnp.where(sub == r, rows[r], block)
        pivot = jnp.where(sub == r, upper[r][r], pivot)
    corner = block
    for r in range(SUB):
        for c in range(r, SUB):
            corner = jnp.where((sub == r) & (lane == first + c), upper[r][c], corner)
    return block, pivot, corner


def eliminate(blocks, b, origin, store):
    count = len(blocks)
    full = blocks[0].shape
    lane = lax.broadcasted_iota(jnp.int32, full, 1)
    sub = lax.broadcasted_iota(jnp.int32, full, 0)
    first = origin + b * SUB
    inside = (lane >= first) & (lane < first + SUB)
    columns = [
        [jnp.broadcast_to(blocks[i][:, first + c : first + c + 1], full) for c in range(SUB)]
        for i in range(b, count)
    ]
    upper = [
        [
            jnp.broadcast_to(columns[0][c][r : r + 1, :], full) if c >= r else None
            for c in range(SUB)
        ]
        for r in range(SUB)
    ]
    rows = [
        jnp.where(
            inside,
            jnp.where(lane == first + r, 1.0, 0.0),
            jnp.broadcast_to(blocks[b][r : r + 1, :], full),
        )
        for r in range(SUB)
    ]
    unit = [[None] * SUB for _ in range(SUB)]
    inverse = [None] * SUB
    for c in range(SUB):
        inverse[c] = 1.0 / upper[c][c]
        for r in range(c + 1, SUB):
            unit[c][r] = upper[c][r] * inverse[c]
            for j in range(r, SUB):
                upper[r][j] = upper[r][j] - unit[c][r] * upper[c][j]
            rows[r] = rows[r] - unit[c][r] * rows[c]
    store(first, rows, upper, lane, sub)
    solved = [rows[r] * inverse[r] for r in range(SUB)]
    for c in range(SUB - 1, 0, -1):
        for r in range(c):
            solved[r] = solved[r] - unit[r][c] * solved[c]
    for i in range(b + 1, count):
        terms = [columns[i - b][c] * solved[c] for c in range(SUB)]
        while len(terms) > 1:
            terms = [terms[t] + terms[t + 1] for t in range(0, len(terms), 2)]
        blocks[i] = jnp.where(inside, 0.0, blocks[i]) - terms[0]


def exact(a, b, dims):
    return lax.dot_general(
        a,
        b,
        (dims, ((), ())),
        precision=lax.Precision.HIGHEST,
        preferred_element_type=jnp.float32,
    )


def basis_kernel(
    points,
    shift,
    spans,
    late_ref,
    early_ref,
    filtered_ref,
    basis_hbm,
    factor_hbm,
    basis_ref,
    factor_ref,
    split,
    turned,
    store_sem,
):
    hours, size = late_ref.shape
    root = math.sqrt(points)
    late = late_ref[...]
    head = early_ref[:hours, :]
    lane = lax.broadcasted_iota(jnp.int32, (hours, size), 1)
    left = lane < hours
    below = exact(late, head, ((1,), (1,)))
    padded = jnp.concatenate([jnp.zeros_like(late), late], axis=0)
    across = jnp.where(left, 0.0, exact(head, padded, ((1,), (1,))))
    state = jnp.where(left, 0.0, late) - exact(below, head + across, ((1,), (0,)))

    def halves(here, inverse):
        begin, end = here
        top = inverse.astype(jnp.bfloat16).astype(jnp.float32)
        split[begin:end, :] = top
        split[size + begin : size + end, :] = inverse - top

    halves((0, hours), head * root)
    turned[:hours, :] = (early_ref[hours:, :] + across) / root

    def store(first, rows, upper, lane, sub):
        block, pivot, corner = assemble(first, rows, upper, lane, sub)
        diagonal = jnp.sqrt(pivot)
        inverse = jnp.where(lane <= sub + first, block, 0.0) * (root / diagonal)
        halves((first, first + SUB), inverse)
        turned[first : first + SUB, :] = jnp.where(lane >= sub + first, corner, 0.0) / (
            diagonal * root
        )

    blocks = [state[SUB * b : SUB * (b + 1), :] for b in range(hours // SUB)]
    for b in range(len(blocks)):
        eliminate(blocks, b, hours, store)
    both_parts = split[...].astype(jnp.bfloat16)
    offset = lax.axis_index("tm") * shift
    stores = []
    for index, (start, width) in enumerate(spans):
        width = min(width, basis_ref.shape[0] - start)
        both = lax.dot_general(
            filtered_ref[pl.ds(pl.multiple_of(offset + start, 2 * SUB), width), :],
            both_parts,
            (((1,), (1,)), ((), ())),
            preferred_element_type=jnp.float32,
        )
        rows = pl.ds(start, width)
        basis_ref[rows, :] = both[:, :size] + both[:, size:]
        copy = pltpu.make_async_copy(
            basis_ref.at[rows], basis_hbm.at[rows], store_sem.at[index]
        )
        copy.start()
        stores.append(copy)
        if index == 0:
            factor_ref[...] = turned[...].T
            copy = pltpu.make_async_copy(factor_ref, factor_hbm, store_sem.at[len(spans)])
            copy.start()
            stores.append(copy)
    for copy in stores:
        copy.wait()


def cut(tiles):
    edge = max(1, tiles // (2 * CHUNKS))
    step = max(1, pl.cdiv(tiles - 2 * edge, CHUNKS - 2))
    cuts = [0, *range(edge, max(edge, tiles - edge), step), max(edge, tiles - edge), tiles]
    return [(a * LANES, (b - a) * LANES) for a, b in zip(cuts, cuts[1:]) if b > a]


def paired_body(thermal_anomaly, smoothing_coefs):
    hours, sites = thermal_anomaly.shape
    total = 2 * hours
    half = sites // 2
    shift = half % LANES
    tiles = pl.cdiv(shift + half, LANES)
    swap_spans = cut(tiles - 1)
    padded = tiles * LANES
    group = PLANE * 2
    lines = lax.axis_size("space") // PLANE
    share = hours // group
    quarter = hours // 2 // PLANE
    dma = pltpu.SemaphoreType.DMA
    vmem = pl.BlockSpec(memory_space=pltpu.VMEM)
    anywhere = pl.BlockSpec(memory_space=pl.ANY)
    filtered, late, early = pl.pallas_call(
        functools.partial(gather_kernel, swap_spans),
        out_shape=(
            jax.ShapeDtypeStruct((padded, total), jnp.bfloat16),
            jax.ShapeDtypeStruct((hours, total), jnp.float32),
            jax.ShapeDtypeStruct((total, total), jnp.float32),
        ),
        in_specs=[pl.BlockSpec(memory_space=pltpu.HBM)] * 2,
        out_specs=(vmem, vmem, vmem),
        scratch_shapes=[
            pltpu.VMEM((hours, sites), jnp.bfloat16),
            pltpu.VMEM((1, total), jnp.float32),
            pltpu.VMEM((hours, LANES), jnp.bfloat16),
            pltpu.VMEM((total, padded), jnp.bfloat16),
            pltpu.VMEM((hours, total), jnp.float32),
            pltpu.VMEM((group - 1, share, total), jnp.float32),
            pltpu.VMEM((share, total), jnp.float32),
            pltpu.VMEM((lines, share, total), jnp.float32),
            pltpu.VMEM((hours // 2, total), jnp.float32),
            pltpu.VMEM((PLANE - 1, quarter, total), jnp.float32),
            pltpu.VMEM((quarter, total), jnp.float32),
            pltpu.VMEM((lines, quarter, total), jnp.float32),
            pltpu.VMEM((hours // 2, total), jnp.float32),
            pltpu.VMEM((hours, total), jnp.float32),
            dma((3,)),
            dma((len(swap_spans) + 1,)),
            dma((len(swap_spans) + 1,)),
            dma((group - 1,)),
            dma((group - 1,)),
            dma((lines - 1,)),
            dma((lines - 1,)),
            dma((group - 1,)),
            dma((group - 1,)),
            dma((PLANE - 1,)),
            dma((PLANE - 1,)),
            dma((lines - 1,)),
            dma((lines - 1,)),
            dma((group,)),
            dma((PLANE,)),
        ],
        compiler_params=pltpu.CompilerParams(
            collective_id=0, has_side_effects=True, vmem_limit_bytes=GRANT
        ),
        name="gather_gram",
    )(
        pltpu.with_memory_space_constraint(thermal_anomaly, pltpu.HBM),
        pltpu.with_memory_space_constraint(smoothing_coefs[:total].reshape(1, total), pltpu.HBM),
    )

    points = sites * lax.axis_size("space")
    spans = cut(pl.cdiv(half, LANES))
    basis, lower = pl.pallas_call(
        functools.partial(basis_kernel, points, shift, spans),
        out_shape=(
            jax.ShapeDtypeStruct((half, total), jnp.float32),
            jax.ShapeDtypeStruct((total, total), jnp.float32),
        ),
        in_specs=[vmem, vmem, vmem],
        out_specs=(anywhere, anywhere),
        scratch_shapes=[
            pltpu.VMEM((half, total), jnp.float32),
            pltpu.VMEM((total, total), jnp.float32),
            pltpu.VMEM((2 * total, total), jnp.float32),
            pltpu.VMEM((total, total), jnp.float32),
            dma((len(spans) + 1,)),
        ],
        compiler_params=pltpu.CompilerParams(vmem_limit_bytes=GRANT),
        name="factor_basis",
    )(late, early, filtered)
    return basis.T, lower


def body(thermal_anomaly, smoothing_coefs):
    hours, sites = thermal_anomaly.shape
    paired = (
        lax.axis_size("tm") == 2
        and 2 * hours == LANES
        and smoothing_coefs.shape[0] >= LANES
        and sites % 2 == 0
        and sites // 2 % LANES % (2 * SUB) == 0
        and sites // 2 > 8 * LANES
        and lax.axis_size("space") % PLANE == 0
        and lax.axis_size("space") > PLANE
    )
    return (paired_body if paired else general_body)(thermal_anomaly, smoothing_coefs)


def solution(mesh):
    placed = (P("tm", "space"), P())
    return jax.shard_map(
        body, mesh=mesh, in_specs=placed, out_specs=(P(None, ("space", "tm")), P()), check_vma=False
    )
```

```python
import functools
import math

import jax
import jax.numpy as jnp
from jax import lax
from jax.experimental import pallas as pl
from jax.experimental.pallas import tpu as pltpu
from jax.sharding import PartitionSpec as P

LANES = 128
SUB = 8
PLANE = 4
CHUNKS = 5
FIRST = 17 * LANES
FAR_FIRST = (7, 5, 3, 1, 6, 4, 2)
NEXT = (1, 4, 2)
LINE_AFTER = 0
GATHER_AFTER = 1
SPLIT = 4
GRANT = 16 * 2**20
MESH = pl.DeviceIdType.MESH


def banded(coefficients, rows, cols, delay):
    lag = (
        lax.broadcasted_iota(jnp.int32, (rows, cols), 0)
        + delay
        - lax.broadcasted_iota(jnp.int32, (rows, cols), 1)
    )
    one_hot = lag[:, :, None] == lax.broadcasted_iota(
        jnp.int32, (1, 1, coefficients.shape[0]), 2
    )
    return jnp.sum(jnp.where(one_hot, coefficients.astype(jnp.float32), 0.0), axis=2).astype(
        coefficients.dtype
    )


def general_body(thermal_anomaly, smoothing_coefs):
    steps = thermal_anomaly.shape[0]
    blocks = lax.axis_size("tm")
    coefficients = jnp.concatenate([jnp.ones((1,), jnp.float32), smoothing_coefs]).astype(
        jnp.bfloat16
    )
    reach = min(blocks - 1, -(-(coefficients.shape[0] - 1) // steps))
    record = [thermal_anomaly]
    for distance in range(1, reach + 1):
        route = [(i, i + distance) for i in range(blocks - distance)]
        record.insert(0, lax.ppermute(thermal_anomaly, "tm", route))
    matrix = banded(coefficients, steps, (reach + 1) * steps, reach * steps)
    outgoing = jnp.dot(
        matrix, jnp.concatenate(record, axis=0), preferred_element_type=jnp.float32
    ).astype(jnp.bfloat16)
    arrived = lax.all_to_all(outgoing, "tm", split_axis=1, concat_axis=0, tiled=True)
    gram = lax.psum(
        jnp.dot(arrived, arrived.T, preferred_element_type=jnp.float32), ("space", "tm")
    )
    lower = jnp.linalg.cholesky(gram)
    rows = jax.scipy.linalg.solve_triangular(lower, arrived.astype(jnp.float32), lower=True)
    scale = jnp.sqrt(jnp.float32(thermal_anomaly.shape[1] * lax.axis_size("space")))
    return rows * scale, lower / scale


def gather_kernel(
    spans,
    x_hbm,
    coef_hbm,
    filtered_ref,
    late_ref,
    early_ref,
    x_ref,
    coef_ref,
    tail,
    panel,
    partial,
    pieces,
    reduced,
    planes,
    first_partial,
    first_pieces,
    first_reduced,
    first_planes,
    first_whole,
    whole,
    load_sem,
    swap_send,
    swap_recv,
    rs_send,
    rs_recv,
    line_send,
    line_recv,
    ag_send,
    ag_recv,
    first_rs_send,
    first_rs_recv,
    first_line_send,
    first_line_recv,
    first_ag_send,
    first_ag_recv,
    mate_sem,
    across_sem,
    along_sem,
):
    space = lax.axis_index("space")
    tm = lax.axis_index("tm")
    inner = space % PLANE
    plane = space // PLANE
    lines = lax.axis_size("space") // PLANE
    group = PLANE * 2
    me = inner * 2 + tm
    hours, sites = x_ref.shape
    total = 2 * hours
    half = sites // 2
    low = half // LANES * LANES
    shift = half - low
    full = panel.shape[1] - LANES
    share = hours // group
    quarter = first_partial.shape[0] // PLANE

    def in_group(k):
        x = inner // 2
        core = inner % 2
        x = 1 - x if k & 4 else x
        core = 1 - core if k & 2 else core
        side = 1 - tm if k & 1 else tm
        near = x * 2 + core
        return near * 2 + side, (plane * PLANE + near, side)

    def in_line(offset):
        return ((plane + offset) % lines * PLANE + inner, tm)

    barrier = pltpu.get_barrier_semaphore()
    for k in NEXT:
        pl.semaphore_signal(barrier, inc=1, device_id=in_group(k)[1], device_id_type=MESH)

    def tell_line(semaphore):
        for step, there in ((-1, plane > 0), (1, plane < lines - 1)):

            @pl.when(there)
            def _():
                pl.semaphore_signal(
                    semaphore,
                    inc=1,
                    device_id=(space + step * PLANE, tm),
                    device_id_type=MESH,
                )

    tell_line(barrier)
    beside = (plane + lines - 1) // lines + (2 * lines - 2 - plane) // lines

    own = pl.ds(pl.multiple_of(tm * hours, hours), hours)
    load_x = pltpu.make_async_copy(x_hbm, x_ref, load_sem.at[0])
    load_coef = pltpu.make_async_copy(coef_hbm, coef_ref, load_sem.at[1])
    load_own = pltpu.make_async_copy(
        x_hbm.at[:, pl.ds(pl.multiple_of(tm * low, LANES), full)],
        panel.at[own, pl.ds(0, full)],
        load_sem.at[2],
    )
    for copy in (load_x, load_coef, load_own):
        copy.start()

    pl.semaphore_wait(barrier, len(NEXT) + beside)
    swaps = []
    for index, (start, width) in enumerate(spans):
        copy = pltpu.make_async_remote_copy(
            src_ref=x_hbm.at[
                :, pl.ds(pl.multiple_of((1 - tm) * low + start, LANES), width)
            ],
            dst_ref=panel.at[own, pl.ds(start, width)],
            send_sem=swap_send.at[index],
            recv_sem=swap_recv.at[index],
            device_id=(space, 1 - tm),
            device_id_type=MESH,
        )
        swaps.append(copy)
    for copy in swaps[:-1]:
        copy.start()
    pl.semaphore_signal(mate_sem, inc=1, device_id=in_group(2)[1], device_id_type=MESH)
    pl.semaphore_wait(mate_sem, 1)
    pl.semaphore_signal(across_sem, inc=1, device_id=in_group(4)[1], device_id_type=MESH)
    for reach in range(lines - 2):
        if reach:
            pl.semaphore_wait(along_sem.at[reach - 1], beside)
        tell_line(along_sem.at[reach])

    load_x.wait()
    for side in range(2):

        @pl.when(tm == side)
        def _():
            for target, to in ((tail, 1 - side), (None, side)):
                begin = to * low + full
                width = min(LANES, sites - begin)
                value = x_ref[:, begin : begin + width]
                if width < LANES:
                    pad = jnp.zeros((hours, LANES - width), value.dtype)
                    value = jnp.concatenate([value, pad], axis=1)
                if target is None:
                    panel[side * hours : (side + 1) * hours, full : full + LANES] = value
                else:
                    target[...] = value

    tail_copy = pltpu.make_async_remote_copy(
        src_ref=tail,
        dst_ref=panel.at[own, pl.ds(full, LANES)],
        send_sem=swap_send.at[len(spans)],
        recv_sem=swap_recv.at[len(spans)],
        device_id=(space, 1 - tm),
        device_id_type=MESH,
    )
    tail_copy.start()
    swaps[-1].start()

    load_coef.wait()
    row = lax.broadcasted_iota(jnp.int32, (total, total), 0)
    col = lax.broadcasted_iota(jnp.int32, (total, total), 1)
    lagged = jnp.broadcast_to(coef_ref[...], (total, total))
    lagged = pltpu.roll(lagged, 1, axis=1, stride=1, stride_axis=0)
    turned = jnp.where(col > row, lagged, jnp.where(col == row, 1.0, 0.0))
    matrix = turned.T.astype(jnp.bfloat16)
    corner = matrix[:hours, :hours]

    def first_near(offset):
        near = (inner + offset) % PLANE
        return near, plane * PLANE + near

    def first_scatter(offset):
        near, other = first_near(offset)
        return pltpu.make_async_remote_copy(
            src_ref=first_partial.at[pl.ds(pl.multiple_of(near * quarter, quarter), quarter)],
            dst_ref=first_pieces.at[offset - 1],
            send_sem=first_rs_send.at[offset - 1],
            recv_sem=first_rs_recv.at[offset - 1],
            device_id=(other, tm),
            device_id_type=MESH,
        )

    def first_line(offset):
        return pltpu.make_async_remote_copy(
            src_ref=first_reduced,
            dst_ref=first_planes.at[plane],
            send_sem=first_line_send.at[offset - 1],
            recv_sem=first_line_recv.at[offset - 1],
            device_id=in_line(offset),
            device_id_type=MESH,
        )

    first_mine = pl.ds(pl.multiple_of(inner * quarter, quarter), quarter)

    def first_gather(offset, side):
        return pltpu.make_async_remote_copy(
            src_ref=first_whole.at[first_mine],
            dst_ref=first_whole.at[first_mine],
            send_sem=first_ag_send.at[side * PLANE + offset],
            recv_sem=first_ag_recv.at[offset],
            device_id=(first_near(offset)[1], side),
            device_id_type=MESH,
        )

    @pl.when(tm == 0)
    def _():
        gram = jnp.zeros((hours, hours), jnp.float32)
        cuts = [*range(0, low + full, FIRST), low + full]
        parts = [x_ref[:, a:b] for a, b in zip(cuts, cuts[1:])] + [tail[...]]
        for part in parts:
            values = jnp.dot(corner, part, preferred_element_type=jnp.float32).astype(jnp.bfloat16)
            gram = gram + lax.dot_general(
                values, values, (((1,), (1,)), ((), ())), preferred_element_type=jnp.float32
            )
        first_partial[...] = jnp.concatenate([gram[: hours // 2], gram[hours // 2 :]], axis=1)
        for offset in range(1, PLANE):
            first_scatter(offset).start()

    def first_stage_line():
        @pl.when(tm == 0)
        def _():
            running = first_partial[first_mine, :]
            for offset in range(1, PLANE):
                first_scatter(offset).wait_recv()
                running = running + first_pieces[offset - 1]
            first_reduced[...] = running
            first_planes[plane] = running
            for offset in range(1, lines):
                first_line(offset).start()

    def first_stage_gather():
        @pl.when(tm == 0)
        def _():
            for offset in range(1, lines):
                first_line(offset).wait_recv()
            running = first_planes[0]
            for index in range(1, lines):
                running = running + first_planes[index]
            first_whole[first_mine, :] = running
            for side in (1, 0):
                for offset in range(PLANE):
                    if side or offset:
                        first_gather(offset, side).start()

    pl.semaphore_wait(across_sem, 1)
    pl.semaphore_wait(along_sem.at[lines - 3], beside)
    load_own.wait()
    partial[...] = jnp.zeros_like(partial)
    for index, (start, width) in enumerate(spans):
        swaps[index].wait_recv()
        if index == len(spans) - 1:
            tail_copy.wait_recv()
            width += LANES
        values = jnp.dot(
            matrix, panel[:, start : start + width], preferred_element_type=jnp.float32
        )
        if start < shift or start + width > half:
            point = lax.broadcasted_iota(jnp.int32, (total, width), 1) + (start - tm * shift)
            values = jnp.where((point >= 0) & (point < half), values, 0.0)
        values = values.astype(jnp.bfloat16)
        if index < len(spans) - 1:
            filtered_ref[start : start + width, :] = values.T
        partial[...] += lax.dot_general(
            values[hours:], values, (((1,), (1,)), ((), ())), preferred_element_type=jnp.float32
        )
        if index == min(LINE_AFTER, len(spans) - 2):
            first_stage_line()
        if index == min(GATHER_AFTER, len(spans) - 2):
            first_stage_gather()

    copies = []
    for k in FAR_FIRST:
        other, device = in_group(k)
        copy = pltpu.make_async_remote_copy(
            src_ref=partial.at[pl.ds(pl.multiple_of(other * share, share), share)],
            dst_ref=pieces.at[k - 1],
            send_sem=rs_send.at[k - 1],
            recv_sem=rs_recv.at[k - 1],
            device_id=device,
            device_id_type=MESH,
        )
        copy.start()
        copies.append(copy)
    filtered_ref[start : start + width, :] = values.T

    @pl.when(tm == 0)
    def _():
        for offset in range(1, PLANE):
            first_gather(offset, 0).wait_recv()

    @pl.when(tm == 1)
    def _():
        for offset in range(PLANE):
            first_gather(offset, 1).wait_recv()

    blank = jnp.zeros((SUB, hours), jnp.float32)
    blocks = []
    for b in range(hours // SUB):
        begin = b * SUB
        packed = first_whole[begin % (hours // 2) : begin % (hours // 2) + SUB, :]
        side = begin // (hours // 2)
        blocks.append(
            jnp.concatenate([packed[:, side * hours : (side + 1) * hours], blank], axis=1)
        )

    def store(first, rows, upper, lane, sub):
        block, pivot, corner = assemble(first, rows, upper, lane, sub)
        diagonal = jnp.sqrt(pivot)
        early_ref[first : first + SUB, :] = (
            jnp.where(lane <= sub + first, block, 0.0) / diagonal
        )
        early_ref[hours + first : hours + first + SUB, :] = (
            jnp.where(lane >= sub + first, corner, 0.0) / diagonal
        )

    for b in range(SPLIT):
        eliminate(blocks, b, 0, store)

    mine = pl.ds(pl.multiple_of(me * share, share), share)
    running = partial[mine, :]
    for k, copy in zip(FAR_FIRST, copies):
        copy.wait_recv()
        running = running + pieces[k - 1]
    reduced[...] = running
    planes[plane] = running

    for offset in range(1, lines):
        copy = pltpu.make_async_remote_copy(
            src_ref=reduced,
            dst_ref=planes.at[plane],
            send_sem=line_send.at[offset - 1],
            recv_sem=line_recv.at[offset - 1],
            device_id=in_line(offset),
            device_id_type=MESH,
        )
        copy.start()
        copies.append(copy)
    for b in range(SPLIT, len(blocks)):
        eliminate(blocks, b, 0, store)
    for copy in copies[group - 1 :]:
        copy.wait_recv()
    running = planes[0]
    for index in range(1, lines):
        running = running + planes[index]
    whole[mine, :] = running

    for k in FAR_FIRST:
        copy = pltpu.make_async_remote_copy(
            src_ref=whole.at[mine],
            dst_ref=whole.at[mine],
            send_sem=ag_send.at[k - 1],
            recv_sem=ag_recv.at[k - 1],
            device_id=in_group(k)[1],
            device_id_type=MESH,
        )
        copy.start()
        copies.append(copy)
    for copy in swaps + [tail_copy] + copies[: -(group - 1)]:
        copy.wait_send()

    @pl.when(tm == 0)
    def _():
        for offset in range(1, PLANE):
            first_scatter(offset).wait_send()
        for offset in range(1, lines):
            first_line(offset).wait_send()
        for side in (1, 0):
            for offset in range(PLANE):
                if side or offset:
                    first_gather(offset, side).wait_send()

    for copy in copies[-(group - 1) :]:
        copy.wait_recv()
    late_ref[...] = whole[...]
    for copy in copies[-(group - 1) :]:
        copy.wait_send()


def assemble(first, rows, upper, lane, sub):
    block = rows[0]
    pivot = upper[0][0]
    for r in range(1, SUB):
        block = jnp.where(sub == r, rows[r], block)
        pivot = jnp.where(sub == r, upper[r][r], pivot)
    corner = block
    for r in range(SUB):
        for c in range(r, SUB):
            corner = jnp.where((sub == r) & (lane == first + c), upper[r][c], corner)
    return block, pivot, corner


def eliminate(blocks, b, origin, store):
    count = len(blocks)
    full = blocks[0].shape
    lane = lax.broadcasted_iota(jnp.int32, full, 1)
    sub = lax.broadcasted_iota(jnp.int32, full, 0)
    first = origin + b * SUB
    inside = (lane >= first) & (lane < first + SUB)
    columns = [
        [jnp.broadcast_to(blocks[i][:, first + c : first + c + 1], full) for c in range(SUB)]
        for i in range(b, count)
    ]
    upper = [
        [
            jnp.broadcast_to(columns[0][c][r : r + 1, :], full) if c >= r else None
            for c in range(SUB)
        ]
        for r in range(SUB)
    ]
    rows = [
        jnp.where(
            inside,
            jnp.where(lane == first + r, 1.0, 0.0),
            jnp.broadcast_to(blocks[b][r : r + 1, :], full),
        )
        for r in range(SUB)
    ]
    unit = [[None] * SUB for _ in range(SUB)]
    inverse = [None] * SUB
    solved = [None] * SUB
    for c in range(SUB):
        inverse[c] = 1.0 / upper[c][c]
        for r in range(c + 1, SUB):
            unit[c][r] = upper[c][r] * inverse[c]
            for j in range(r, SUB):
                upper[r][j] = upper[r][j] - unit[c][r] * upper[c][j]
            rows[r] = rows[r] - unit[c][r] * rows[c]
        solved[c] = rows[c] * inverse[c]
        for r in range(c):
            solved[r] = solved[r] - unit[r][c] * solved[c]
            for j in range(c + 1, SUB):
                unit[r][j] = unit[r][j] - unit[r][c] * unit[c][j]
    store(first, rows, upper, lane, sub)
    for i in range(b + 1, count):
        terms = [columns[i - b][c] * solved[c] for c in range(SUB)]
        while len(terms) > 1:
            terms = [terms[t] + terms[t + 1] for t in range(0, len(terms), 2)]
        blocks[i] = jnp.where(inside, 0.0, blocks[i]) - terms[0]


def exact(a, b, dims):
    return lax.dot_general(
        a,
        b,
        (dims, ((), ())),
        precision=lax.Precision.HIGHEST,
        preferred_element_type=jnp.float32,
    )


def basis_kernel(
    points,
    shift,
    spans,
    late_ref,
    early_ref,
    filtered_ref,
    basis_hbm,
    factor_hbm,
    basis_ref,
    factor_ref,
    split,
    turned,
    store_sem,
):
    hours, size = late_ref.shape
    root = math.sqrt(points)
    late = late_ref[...]
    head = early_ref[:hours, :]
    lane = lax.broadcasted_iota(jnp.int32, (hours, size), 1)
    left = lane < hours
    below = exact(late, head, ((1,), (1,)))
    padded = jnp.concatenate([jnp.zeros_like(late), late], axis=0)
    across = jnp.where(left, 0.0, exact(head, padded, ((1,), (1,))))
    state = jnp.where(left, 0.0, late) - exact(below, head + across, ((1,), (0,)))

    def halves(here, inverse):
        begin, end = here
        top = inverse.astype(jnp.bfloat16).astype(jnp.float32)
        split[begin:end, :] = top
        split[size + begin : size + end, :] = inverse - top

    halves((0, hours), head * root)
    turned[:hours, :] = (early_ref[hours:, :] + across) / root

    def store(first, rows, upper, lane, sub):
        block, pivot, corner = assemble(first, rows, upper, lane, sub)
        diagonal = jnp.sqrt(pivot)
        inverse = jnp.where(lane <= sub + first, block, 0.0) * (root / diagonal)
        halves((first, first + SUB), inverse)
        turned[first : first + SUB, :] = jnp.where(lane >= sub + first, corner, 0.0) / (
            diagonal * root
        )

    blocks = [state[SUB * b : SUB * (b + 1), :] for b in range(hours // SUB)]
    for b in range(len(blocks)):
        eliminate(blocks, b, hours, store)
    both_parts = split[...].astype(jnp.bfloat16)
    offset = lax.axis_index("tm") * shift
    stores = []
    for index, (start, width) in enumerate(spans):
        width = min(width, basis_ref.shape[0] - start)
        both = lax.dot_general(
            filtered_ref[pl.ds(pl.multiple_of(offset + start, 2 * SUB), width), :],
            both_parts,
            (((1,), (1,)), ((), ())),
            preferred_element_type=jnp.float32,
        )
        rows = pl.ds(start, width)
        basis_ref[rows, :] = both[:, :size] + both[:, size:]
        copy = pltpu.make_async_copy(
            basis_ref.at[rows], basis_hbm.at[rows], store_sem.at[index]
        )
        copy.start()
        stores.append(copy)
        if index == 0:
            factor_ref[...] = turned[...].T
            copy = pltpu.make_async_copy(factor_ref, factor_hbm, store_sem.at[len(spans)])
            copy.start()
            stores.append(copy)
    for copy in stores:
        copy.wait()


def cut(tiles):
    edge = max(1, tiles // (2 * CHUNKS))
    step = max(1, pl.cdiv(tiles - 2 * edge, CHUNKS - 2))
    cuts = [0, *range(edge, max(edge, tiles - edge), step), max(edge, tiles - edge), tiles]
    return [(a * LANES, (b - a) * LANES) for a, b in zip(cuts, cuts[1:]) if b > a]


def paired_body(thermal_anomaly, smoothing_coefs):
    hours, sites = thermal_anomaly.shape
    total = 2 * hours
    half = sites // 2
    shift = half % LANES
    tiles = pl.cdiv(shift + half, LANES)
    swap_spans = cut(tiles - 1)
    padded = tiles * LANES
    group = PLANE * 2
    lines = lax.axis_size("space") // PLANE
    share = hours // group
    quarter = hours // 2 // PLANE
    dma = pltpu.SemaphoreType.DMA
    vmem = pl.BlockSpec(memory_space=pltpu.VMEM)
    anywhere = pl.BlockSpec(memory_space=pl.ANY)
    filtered, late, early = pl.pallas_call(
        functools.partial(gather_kernel, swap_spans),
        out_shape=(
            jax.ShapeDtypeStruct((padded, total), jnp.bfloat16),
            jax.ShapeDtypeStruct((hours, total), jnp.float32),
            jax.ShapeDtypeStruct((total, total), jnp.float32),
        ),
        in_specs=[pl.BlockSpec(memory_space=pltpu.HBM)] * 2,
        out_specs=(vmem, vmem, vmem),
        scratch_shapes=[
            pltpu.VMEM((hours, sites), jnp.bfloat16),
            pltpu.VMEM((1, total), jnp.float32),
            pltpu.VMEM((hours, LANES), jnp.bfloat16),
            pltpu.VMEM((total, padded), jnp.bfloat16),
            pltpu.VMEM((hours, total), jnp.float32),
            pltpu.VMEM((group - 1, share, total), jnp.float32),
            pltpu.VMEM((share, total), jnp.float32),
            pltpu.VMEM((lines, share, total), jnp.float32),
            pltpu.VMEM((hours // 2, total), jnp.float32),
            pltpu.VMEM((PLANE - 1, quarter, total), jnp.float32),
            pltpu.VMEM((quarter, total), jnp.float32),
            pltpu.VMEM((lines, quarter, total), jnp.float32),
            pltpu.VMEM((hours // 2, total), jnp.float32),
            pltpu.VMEM((hours, total), jnp.float32),
            dma((3,)),
            dma((len(swap_spans) + 1,)),
            dma((len(swap_spans) + 1,)),
            dma((group - 1,)),
            dma((group - 1,)),
            dma((lines - 1,)),
            dma((lines - 1,)),
            dma((group - 1,)),
            dma((group - 1,)),
            dma((PLANE - 1,)),
            dma((PLANE - 1,)),
            dma((lines - 1,)),
            dma((lines - 1,)),
            dma((group,)),
            dma((PLANE,)),
            pltpu.SemaphoreType.REGULAR,
            pltpu.SemaphoreType.REGULAR,
            pltpu.SemaphoreType.REGULAR((lines - 2,)),
        ],
        compiler_params=pltpu.CompilerParams(
            collective_id=0, has_side_effects=True, vmem_limit_bytes=GRANT
        ),
        name="gather_gram",
    )(
        pltpu.with_memory_space_constraint(thermal_anomaly, pltpu.HBM),
        pltpu.with_memory_space_constraint(smoothing_coefs[:total].reshape(1, total), pltpu.HBM),
    )

    points = sites * lax.axis_size("space")
    spans = cut(pl.cdiv(half, LANES))
    basis, lower = pl.pallas_call(
        functools.partial(basis_kernel, points, shift, spans),
        out_shape=(
            jax.ShapeDtypeStruct((half, total), jnp.float32),
            jax.ShapeDtypeStruct((total, total), jnp.float32),
        ),
        in_specs=[vmem, vmem, vmem],
        out_specs=(anywhere, anywhere),
        scratch_shapes=[
            pltpu.VMEM((half, total), jnp.float32),
            pltpu.VMEM((total, total), jnp.float32),
            pltpu.VMEM((2 * total, total), jnp.float32),
            pltpu.VMEM((total, total), jnp.float32),
            dma((len(spans) + 1,)),
        ],
        compiler_params=pltpu.CompilerParams(vmem_limit_bytes=GRANT),
        name="factor_basis",
    )(late, early, filtered)
    return basis.T, lower


def body(thermal_anomaly, smoothing_coefs):
    hours, sites = thermal_anomaly.shape
    paired = (
        lax.axis_size("tm") == 2
        and 2 * hours == LANES
        and smoothing_coefs.shape[0] >= LANES
        and sites % 2 == 0
        and sites // 2 % LANES % (2 * SUB) == 0
        and sites // 2 > 8 * LANES
        and lax.axis_size("space") % PLANE == 0
        and lax.axis_size("space") > 2 * PLANE
    )
    return (paired_body if paired else general_body)(thermal_anomaly, smoothing_coefs)


def solution(mesh):
    placed = (P("tm", "space"), P())
    return jax.shard_map(
        body, mesh=mesh, in_specs=placed, out_specs=(P(None, ("space", "tm")), P()), check_vma=False
    )
```

```python
import functools
import math

import jax
import jax.numpy as jnp
from jax import lax
from jax.experimental import pallas as pl
from jax.experimental.pallas import tpu as pltpu
from jax.sharding import PartitionSpec as P

LANES = 128
SUB = 8
PLANE = 4
CHUNKS = 5
FIRST = 17 * LANES
FAR_FIRST = (7, 5, 3, 1, 6, 4, 2)
NEXT = (1, 2)
LINE_AFTER = 1
GATHER_AFTER = 2
SPLIT = 4
GRANT = 16 * 2**20
MESH = pl.DeviceIdType.MESH


def banded(coefficients, rows, cols, delay):
    lag = (
        lax.broadcasted_iota(jnp.int32, (rows, cols), 0)
        + delay
        - lax.broadcasted_iota(jnp.int32, (rows, cols), 1)
    )
    one_hot = lag[:, :, None] == lax.broadcasted_iota(
        jnp.int32, (1, 1, coefficients.shape[0]), 2
    )
    return jnp.sum(jnp.where(one_hot, coefficients.astype(jnp.float32), 0.0), axis=2).astype(
        coefficients.dtype
    )


def general_body(thermal_anomaly, smoothing_coefs):
    steps = thermal_anomaly.shape[0]
    blocks = lax.axis_size("tm")
    coefficients = jnp.concatenate([jnp.ones((1,), jnp.float32), smoothing_coefs]).astype(
        jnp.bfloat16
    )
    reach = min(blocks - 1, -(-(coefficients.shape[0] - 1) // steps))
    record = [thermal_anomaly]
    for distance in range(1, reach + 1):
        route = [(i, i + distance) for i in range(blocks - distance)]
        record.insert(0, lax.ppermute(thermal_anomaly, "tm", route))
    matrix = banded(coefficients, steps, (reach + 1) * steps, reach * steps)
    outgoing = jnp.dot(
        matrix, jnp.concatenate(record, axis=0), preferred_element_type=jnp.float32
    ).astype(jnp.bfloat16)
    arrived = lax.all_to_all(outgoing, "tm", split_axis=1, concat_axis=0, tiled=True)
    gram = lax.psum(
        jnp.dot(arrived, arrived.T, preferred_element_type=jnp.float32), ("space", "tm")
    )
    lower = jnp.linalg.cholesky(gram)
    rows = jax.scipy.linalg.solve_triangular(lower, arrived.astype(jnp.float32), lower=True)
    scale = jnp.sqrt(jnp.float32(thermal_anomaly.shape[1] * lax.axis_size("space")))
    return rows * scale, lower / scale


def gather_kernel(
    spans,
    x_hbm,
    coef_hbm,
    filtered_ref,
    late_ref,
    early_ref,
    x_ref,
    coef_ref,
    tail,
    panel,
    partial,
    pieces,
    reduced,
    planes,
    first_partial,
    first_pieces,
    first_reduced,
    first_planes,
    first_whole,
    whole,
    load_sem,
    swap_send,
    swap_recv,
    rs_send,
    rs_recv,
    line_send,
    line_recv,
    ag_send,
    ag_recv,
    first_rs_send,
    first_rs_recv,
    first_line_send,
    first_line_recv,
    first_ag_send,
    first_ag_recv,
    know_sem,
    all_sem,
    along_sem,
):
    space = lax.axis_index("space")
    tm = lax.axis_index("tm")
    inner = space % PLANE
    plane = space // PLANE
    lines = lax.axis_size("space") // PLANE
    group = PLANE * 2
    me = inner * 2 + tm
    hours, sites = x_ref.shape
    total = 2 * hours
    half = sites // 2
    low = half // LANES * LANES
    shift = half - low
    full = panel.shape[1] - LANES
    share = hours // group
    quarter = first_partial.shape[0] // PLANE

    def in_group(k):
        x = inner // 2
        core = inner % 2
        x = 1 - x if k & 4 else x
        core = 1 - core if k & 2 else core
        side = 1 - tm if k & 1 else tm
        near = x * 2 + core
        return near * 2 + side, (plane * PLANE + near, side)

    def in_line(offset):
        return ((plane + offset) % lines * PLANE + inner, tm)

    barrier = pltpu.get_barrier_semaphore()
    for k in NEXT:
        pl.semaphore_signal(barrier, inc=1, device_id=in_group(k)[1], device_id_type=MESH)

    def tell_line(semaphore):
        for step, there in ((-1, plane > 0), (1, plane < lines - 1)):

            @pl.when(there)
            def _():
                pl.semaphore_signal(
                    semaphore,
                    inc=1,
                    device_id=(space + step * PLANE, tm),
                    device_id_type=MESH,
                )

    tell_line(barrier)

    @pl.when(plane == 0)
    def _():
        pl.semaphore_signal(barrier, inc=1, device_id=in_group(4)[1], device_id_type=MESH)

    beside = (plane + lines - 1) // lines + (2 * lines - 2 - plane) // lines

    own = pl.ds(pl.multiple_of(tm * hours, hours), hours)
    load_x = pltpu.make_async_copy(x_hbm, x_ref, load_sem.at[0])
    load_coef = pltpu.make_async_copy(coef_hbm, coef_ref, load_sem.at[1])
    load_own = pltpu.make_async_copy(
        x_hbm.at[:, pl.ds(pl.multiple_of(tm * low, LANES), full)],
        panel.at[own, pl.ds(0, full)],
        load_sem.at[2],
    )
    for copy in (load_x, load_coef, load_own):
        copy.start()

    pl.semaphore_wait(barrier, len(NEXT) + beside + (lines - 1 - plane) // (lines - 1))
    swaps = []
    for index, (start, width) in enumerate(spans):
        copy = pltpu.make_async_remote_copy(
            src_ref=x_hbm.at[
                :, pl.ds(pl.multiple_of((1 - tm) * low + start, LANES), width)
            ],
            dst_ref=panel.at[own, pl.ds(start, width)],
            send_sem=swap_send.at[index],
            recv_sem=swap_recv.at[index],
            device_id=(space, 1 - tm),
            device_id_type=MESH,
        )
        swaps.append(copy)
    for copy in swaps[:-1]:
        copy.start()

    load_x.wait()
    for side in range(2):

        @pl.when(tm == side)
        def _():
            for target, to in ((tail, 1 - side), (None, side)):
                begin = to * low + full
                width = min(LANES, sites - begin)
                value = x_ref[:, begin : begin + width]
                if width < LANES:
                    pad = jnp.zeros((hours, LANES - width), value.dtype)
                    value = jnp.concatenate([value, pad], axis=1)
                if target is None:
                    panel[side * hours : (side + 1) * hours, full : full + LANES] = value
                else:
                    target[...] = value

    tail_copy = pltpu.make_async_remote_copy(
        src_ref=tail,
        dst_ref=panel.at[own, pl.ds(full, LANES)],
        send_sem=swap_send.at[len(spans)],
        recv_sem=swap_recv.at[len(spans)],
        device_id=(space, 1 - tm),
        device_id_type=MESH,
    )
    tail_copy.start()
    swaps[-1].start()
    for reach in range(lines - 2):
        if reach:
            pl.semaphore_wait(along_sem.at[reach - 1], beside)
        tell_line(along_sem.at[reach])

    load_coef.wait()
    row = lax.broadcasted_iota(jnp.int32, (total, total), 0)
    col = lax.broadcasted_iota(jnp.int32, (total, total), 1)
    lagged = jnp.broadcast_to(coef_ref[...], (total, total))
    lagged = pltpu.roll(lagged, 1, axis=1, stride=1, stride_axis=0)
    turned = jnp.where(col > row, lagged, jnp.where(col == row, 1.0, 0.0))
    matrix = turned.T.astype(jnp.bfloat16)
    corner = matrix[:hours, :hours]

    def first_near(offset):
        near = (inner + offset) % PLANE
        return near, plane * PLANE + near

    def first_scatter(offset):
        near, other = first_near(offset)
        return pltpu.make_async_remote_copy(
            src_ref=first_partial.at[pl.ds(pl.multiple_of(near * quarter, quarter), quarter)],
            dst_ref=first_pieces.at[offset - 1],
            send_sem=first_rs_send.at[offset - 1],
            recv_sem=first_rs_recv.at[offset - 1],
            device_id=(other, tm),
            device_id_type=MESH,
        )

    def first_line(offset):
        return pltpu.make_async_remote_copy(
            src_ref=first_reduced,
            dst_ref=first_planes.at[plane],
            send_sem=first_line_send.at[offset - 1],
            recv_sem=first_line_recv.at[offset - 1],
            device_id=in_line(offset),
            device_id_type=MESH,
        )

    first_mine = pl.ds(pl.multiple_of(inner * quarter, quarter), quarter)

    def first_gather(offset, side):
        return pltpu.make_async_remote_copy(
            src_ref=first_whole.at[first_mine],
            dst_ref=first_whole.at[first_mine],
            send_sem=first_ag_send.at[side * PLANE + offset],
            recv_sem=first_ag_recv.at[offset],
            device_id=(first_near(offset)[1], side),
            device_id_type=MESH,
        )

    @pl.when(tm == 0)
    def _():
        gram = jnp.zeros((hours, hours), jnp.float32)
        cuts = [*range(0, low + full, FIRST), low + full]
        parts = [x_ref[:, a:b] for a, b in zip(cuts, cuts[1:])] + [tail[...]]
        for part in parts:
            values = jnp.dot(corner, part, preferred_element_type=jnp.float32).astype(jnp.bfloat16)
            gram = gram + lax.dot_general(
                values, values, (((1,), (1,)), ((), ())), preferred_element_type=jnp.float32
            )
        first_partial[...] = jnp.concatenate([gram[: hours // 2], gram[hours // 2 :]], axis=1)

    def first_stage_scatter():
        pl.semaphore_wait(along_sem.at[lines - 3], beside)

        @pl.when(plane == 0)
        def _():
            for index, k in enumerate((1, 2, 4)):
                pl.semaphore_signal(
                    know_sem.at[index],
                    inc=1,
                    device_id=in_group(k)[1],
                    device_id_type=MESH,
                )
                pl.semaphore_wait(know_sem.at[index], 1)
            for offset in range(1, lines):
                pl.semaphore_signal(
                    all_sem, inc=1, device_id=in_line(offset), device_id_type=MESH
                )

        @pl.when(plane > 0)
        def _():
            pl.semaphore_wait(all_sem, 1)

        @pl.when(tm == 0)
        def _():
            for offset in range(1, PLANE):
                first_scatter(offset).start()

    def first_stage_line():
        @pl.when(tm == 0)
        def _():
            running = first_partial[first_mine, :]
            for offset in range(1, PLANE):
                first_scatter(offset).wait_recv()
                running = running + first_pieces[offset - 1]
            first_reduced[...] = running
            first_planes[plane] = running
            for offset in range(1, lines):
                first_line(offset).start()

    def first_stage_gather():
        @pl.when(tm == 0)
        def _():
            for offset in range(1, lines):
                first_line(offset).wait_recv()
            running = first_planes[0]
            for index in range(1, lines):
                running = running + first_planes[index]
            first_whole[first_mine, :] = running
            for side in (1, 0):
                for offset in range(PLANE):
                    if side or offset:
                        first_gather(offset, side).start()

    load_own.wait()
    partial[...] = jnp.zeros_like(partial)
    for index, (start, width) in enumerate(spans):
        swaps[index].wait_recv()
        if index == len(spans) - 1:
            tail_copy.wait_recv()
            width += LANES
        values = jnp.dot(
            matrix, panel[:, start : start + width], preferred_element_type=jnp.float32
        )
        if start < shift or start + width > half:
            point = lax.broadcasted_iota(jnp.int32, (total, width), 1) + (start - tm * shift)
            values = jnp.where((point >= 0) & (point < half), values, 0.0)
        values = values.astype(jnp.bfloat16)
        if index < len(spans) - 1:
            filtered_ref[start : start + width, :] = values.T
        partial[...] += lax.dot_general(
            values[hours:], values, (((1,), (1,)), ((), ())), preferred_element_type=jnp.float32
        )
        if index == 0:
            first_stage_scatter()
        if index == min(LINE_AFTER, len(spans) - 2):
            first_stage_line()
        if index == min(GATHER_AFTER, len(spans) - 2):
            first_stage_gather()

    copies = []
    for k in FAR_FIRST:
        other, device = in_group(k)
        copy = pltpu.make_async_remote_copy(
            src_ref=partial.at[pl.ds(pl.multiple_of(other * share, share), share)],
            dst_ref=pieces.at[k - 1],
            send_sem=rs_send.at[k - 1],
            recv_sem=rs_recv.at[k - 1],
            device_id=device,
            device_id_type=MESH,
        )
        copy.start()
        copies.append(copy)
    filtered_ref[start : start + width, :] = values.T

    @pl.when(tm == 0)
    def _():
        for offset in range(1, PLANE):
            first_gather(offset, 0).wait_recv()

    @pl.when(tm == 1)
    def _():
        for offset in range(PLANE):
            first_gather(offset, 1).wait_recv()

    blank = jnp.zeros((SUB, hours), jnp.float32)
    blocks = []
    for b in range(hours // SUB):
        begin = b * SUB
        packed = first_whole[begin % (hours // 2) : begin % (hours // 2) + SUB, :]
        side = begin // (hours // 2)
        blocks.append(
            jnp.concatenate([packed[:, side * hours : (side + 1) * hours], blank], axis=1)
        )

    def store(first, rows, upper, lane, sub):
        block, pivot, corner = assemble(first, rows, upper, lane, sub)
        diagonal = jnp.sqrt(pivot)
        early_ref[first : first + SUB, :] = (
            jnp.where(lane <= sub + first, block, 0.0) / diagonal
        )
        early_ref[hours + first : hours + first + SUB, :] = (
            jnp.where(lane >= sub + first, corner, 0.0) / diagonal
        )

    for b in range(SPLIT):
        eliminate(blocks, b, 0, store)

    mine = pl.ds(pl.multiple_of(me * share, share), share)
    running = partial[mine, :]
    for k, copy in zip(FAR_FIRST, copies):
        copy.wait_recv()
        running = running + pieces[k - 1]
    reduced[...] = running
    planes[plane] = running

    for offset in range(1, lines):
        copy = pltpu.make_async_remote_copy(
            src_ref=reduced,
            dst_ref=planes.at[plane],
            send_sem=line_send.at[offset - 1],
            recv_sem=line_recv.at[offset - 1],
            device_id=in_line(offset),
            device_id_type=MESH,
        )
        copy.start()
        copies.append(copy)
    for b in range(SPLIT, len(blocks)):
        eliminate(blocks, b, 0, store)
    for copy in copies[group - 1 :]:
        copy.wait_recv()
    running = planes[0]
    for index in range(1, lines):
        running = running + planes[index]
    whole[mine, :] = running

    for k in FAR_FIRST:
        copy = pltpu.make_async_remote_copy(
            src_ref=whole.at[mine],
            dst_ref=whole.at[mine],
            send_sem=ag_send.at[k - 1],
            recv_sem=ag_recv.at[k - 1],
            device_id=in_group(k)[1],
            device_id_type=MESH,
        )
        copy.start()
        copies.append(copy)
    for copy in swaps + [tail_copy] + copies[: -(group - 1)]:
        copy.wait_send()

    @pl.when(tm == 0)
    def _():
        for offset in range(1, PLANE):
            first_scatter(offset).wait_send()
        for offset in range(1, lines):
            first_line(offset).wait_send()
        for side in (1, 0):
            for offset in range(PLANE):
                if side or offset:
                    first_gather(offset, side).wait_send()

    for copy in copies[-(group - 1) :]:
        copy.wait_recv()
    late_ref[...] = whole[...]
    for copy in copies[-(group - 1) :]:
        copy.wait_send()


def assemble(first, rows, upper, lane, sub):
    block = rows[0]
    pivot = upper[0][0]
    for r in range(1, SUB):
        block = jnp.where(sub == r, rows[r], block)
        pivot = jnp.where(sub == r, upper[r][r], pivot)
    corner = block
    for r in range(SUB):
        for c in range(r, SUB):
            corner = jnp.where((sub == r) & (lane == first + c), upper[r][c], corner)
    return block, pivot, corner


def eliminate(blocks, b, origin, store):
    count = len(blocks)
    full = blocks[0].shape
    lane = lax.broadcasted_iota(jnp.int32, full, 1)
    sub = lax.broadcasted_iota(jnp.int32, full, 0)
    first = origin + b * SUB
    inside = (lane >= first) & (lane < first + SUB)
    columns = [
        [jnp.broadcast_to(blocks[i][:, first + c : first + c + 1], full) for c in range(SUB)]
        for i in range(b, count)
    ]
    upper = [
        [
            jnp.broadcast_to(columns[0][c][r : r + 1, :], full) if c >= r else None
            for c in range(SUB)
        ]
        for r in range(SUB)
    ]
    rows = [
        jnp.where(
            inside,
            jnp.where(lane == first + r, 1.0, 0.0),
            jnp.broadcast_to(blocks[b][r : r + 1, :], full),
        )
        for r in range(SUB)
    ]
    unit = [[None] * SUB for _ in range(SUB)]
    inverse = [None] * SUB
    solved = [None] * SUB
    for c in range(SUB):
        inverse[c] = 1.0 / upper[c][c]
        for r in range(c + 1, SUB):
            unit[c][r] = upper[c][r] * inverse[c]
            for j in range(r, SUB):
                upper[r][j] = upper[r][j] - unit[c][r] * upper[c][j]
            rows[r] = rows[r] - unit[c][r] * rows[c]
        solved[c] = rows[c] * inverse[c]
        for r in range(c):
            solved[r] = solved[r] - unit[r][c] * solved[c]
            for j in range(c + 1, SUB):
                unit[r][j] = unit[r][j] - unit[r][c] * unit[c][j]
    store(first, rows, upper, lane, sub)
    for i in range(b + 1, count):
        terms = [columns[i - b][c] * solved[c] for c in range(SUB)]
        while len(terms) > 1:
            terms = [terms[t] + terms[t + 1] for t in range(0, len(terms), 2)]
        blocks[i] = jnp.where(inside, 0.0, blocks[i]) - terms[0]


def exact(a, b, dims):
    return lax.dot_general(
        a,
        b,
        (dims, ((), ())),
        precision=lax.Precision.HIGHEST,
        preferred_element_type=jnp.float32,
    )


def basis_kernel(
    points,
    shift,
    spans,
    late_ref,
    early_ref,
    filtered_ref,
    basis_hbm,
    factor_hbm,
    basis_ref,
    factor_ref,
    split,
    turned,
    store_sem,
):
    hours, size = late_ref.shape
    root = math.sqrt(points)
    late = late_ref[...]
    head = early_ref[:hours, :]
    lane = lax.broadcasted_iota(jnp.int32, (hours, size), 1)
    left = lane < hours
    below = exact(late, head, ((1,), (1,)))
    padded = jnp.concatenate([jnp.zeros_like(late), late], axis=0)
    across = jnp.where(left, 0.0, exact(head, padded, ((1,), (1,))))
    state = jnp.where(left, 0.0, late) - exact(below, head + across, ((1,), (0,)))

    def halves(here, inverse):
        begin, end = here
        top = inverse.astype(jnp.bfloat16).astype(jnp.float32)
        split[begin:end, :] = top
        split[size + begin : size + end, :] = inverse - top

    halves((0, hours), head * root)
    turned[:hours, :] = (early_ref[hours:, :] + across) / root

    def store(first, rows, upper, lane, sub):
        block, pivot, corner = assemble(first, rows, upper, lane, sub)
        diagonal = jnp.sqrt(pivot)
        inverse = jnp.where(lane <= sub + first, block, 0.0) * (root / diagonal)
        halves((first, first + SUB), inverse)
        turned[first : first + SUB, :] = jnp.where(lane >= sub + first, corner, 0.0) / (
            diagonal * root
        )

    blocks = [state[SUB * b : SUB * (b + 1), :] for b in range(hours // SUB)]
    for b in range(len(blocks)):
        eliminate(blocks, b, hours, store)
    both_parts = split[...].astype(jnp.bfloat16)
    offset = lax.axis_index("tm") * shift
    stores = []
    for index, (start, width) in enumerate(spans):
        width = min(width, basis_ref.shape[0] - start)
        both = lax.dot_general(
            filtered_ref[pl.ds(pl.multiple_of(offset + start, 2 * SUB), width), :],
            both_parts,
            (((1,), (1,)), ((), ())),
            preferred_element_type=jnp.float32,
        )
        rows = pl.ds(start, width)
        basis_ref[rows, :] = both[:, :size] + both[:, size:]
        copy = pltpu.make_async_copy(
            basis_ref.at[rows], basis_hbm.at[rows], store_sem.at[index]
        )
        copy.start()
        stores.append(copy)
        if index == 0:
            factor_ref[...] = turned[...].T
            copy = pltpu.make_async_copy(factor_ref, factor_hbm, store_sem.at[len(spans)])
            copy.start()
            stores.append(copy)
    for copy in stores:
        copy.wait()


def cut(tiles):
    edge = max(1, tiles // (2 * CHUNKS))
    step = max(1, pl.cdiv(tiles - 2 * edge, CHUNKS - 2))
    cuts = [0, *range(edge, max(edge, tiles - edge), step), max(edge, tiles - edge), tiles]
    return [(a * LANES, (b - a) * LANES) for a, b in zip(cuts, cuts[1:]) if b > a]


def paired_body(thermal_anomaly, smoothing_coefs):
    hours, sites = thermal_anomaly.shape
    total = 2 * hours
    half = sites // 2
    shift = half % LANES
    tiles = pl.cdiv(shift + half, LANES)
    swap_spans = cut(tiles - 1)
    padded = tiles * LANES
    group = PLANE * 2
    lines = lax.axis_size("space") // PLANE
    share = hours // group
    quarter = hours // 2 // PLANE
    dma = pltpu.SemaphoreType.DMA
    vmem = pl.BlockSpec(memory_space=pltpu.VMEM)
    anywhere = pl.BlockSpec(memory_space=pl.ANY)
    filtered, late, early = pl.pallas_call(
        functools.partial(gather_kernel, swap_spans),
        out_shape=(
            jax.ShapeDtypeStruct((padded, total), jnp.bfloat16),
            jax.ShapeDtypeStruct((hours, total), jnp.float32),
            jax.ShapeDtypeStruct((total, total), jnp.float32),
        ),
        in_specs=[pl.BlockSpec(memory_space=pltpu.HBM)] * 2,
        out_specs=(vmem, vmem, vmem),
        scratch_shapes=[
            pltpu.VMEM((hours, sites), jnp.bfloat16),
            pltpu.VMEM((1, total), jnp.float32),
            pltpu.VMEM((hours, LANES), jnp.bfloat16),
            pltpu.VMEM((total, padded), jnp.bfloat16),
            pltpu.VMEM((hours, total), jnp.float32),
            pltpu.VMEM((group - 1, share, total), jnp.float32),
            pltpu.VMEM((share, total), jnp.float32),
            pltpu.VMEM((lines, share, total), jnp.float32),
            pltpu.VMEM((hours // 2, total), jnp.float32),
            pltpu.VMEM((PLANE - 1, quarter, total), jnp.float32),
            pltpu.VMEM((quarter, total), jnp.float32),
            pltpu.VMEM((lines, quarter, total), jnp.float32),
            pltpu.VMEM((hours // 2, total), jnp.float32),
            pltpu.VMEM((hours, total), jnp.float32),
            dma((3,)),
            dma((len(swap_spans) + 1,)),
            dma((len(swap_spans) + 1,)),
            dma((group - 1,)),
            dma((group - 1,)),
            dma((lines - 1,)),
            dma((lines - 1,)),
            dma((group - 1,)),
            dma((group - 1,)),
            dma((PLANE - 1,)),
            dma((PLANE - 1,)),
            dma((lines - 1,)),
            dma((lines - 1,)),
            dma((group,)),
            dma((PLANE,)),
            pltpu.SemaphoreType.REGULAR((3,)),
            pltpu.SemaphoreType.REGULAR,
            pltpu.SemaphoreType.REGULAR((lines - 2,)),
        ],
        compiler_params=pltpu.CompilerParams(
            collective_id=0, has_side_effects=True, vmem_limit_bytes=GRANT
        ),
        name="gather_gram",
    )(
        pltpu.with_memory_space_constraint(thermal_anomaly, pltpu.HBM),
        pltpu.with_memory_space_constraint(smoothing_coefs[:total].reshape(1, total), pltpu.HBM),
    )

    points = sites * lax.axis_size("space")
    spans = cut(pl.cdiv(half, LANES))
    basis, lower = pl.pallas_call(
        functools.partial(basis_kernel, points, shift, spans),
        out_shape=(
            jax.ShapeDtypeStruct((half, total), jnp.float32),
            jax.ShapeDtypeStruct((total, total), jnp.float32),
        ),
        in_specs=[vmem, vmem, vmem],
        out_specs=(anywhere, anywhere),
        scratch_shapes=[
            pltpu.VMEM((half, total), jnp.float32),
            pltpu.VMEM((total, total), jnp.float32),
            pltpu.VMEM((2 * total, total), jnp.float32),
            pltpu.VMEM((total, total), jnp.float32),
            dma((len(spans) + 1,)),
        ],
        compiler_params=pltpu.CompilerParams(vmem_limit_bytes=GRANT),
        name="factor_basis",
    )(late, early, filtered)
    return basis.T, lower


def body(thermal_anomaly, smoothing_coefs):
    hours, sites = thermal_anomaly.shape
    paired = (
        lax.axis_size("tm") == 2
        and 2 * hours == LANES
        and smoothing_coefs.shape[0] >= LANES
        and sites % 2 == 0
        and sites // 2 % LANES % (2 * SUB) == 0
        and sites // 2 > 8 * LANES
        and lax.axis_size("space") % PLANE == 0
        and lax.axis_size("space") > 2 * PLANE
    )
    return (paired_body if paired else general_body)(thermal_anomaly, smoothing_coefs)


def solution(mesh):
    placed = (P("tm", "space"), P())
    return jax.shard_map(
        body, mesh=mesh, in_specs=placed, out_specs=(P(None, ("space", "tm")), P()), check_vma=False
    )
```
